512 devices in a mesh: dp: 8 (over z), uly: 8 (over y_lo, core), blk: 8 (over x, y_hi).
Axes of the slice: x: 4, y: 8 (y_hi: 2, y_lo: 4; y = y_hi * 4 + y_lo), z: 8, core: 2. Of those that a mesh axis runs over, the one named last changes fastest.
Arguments:
- query_rows: bfloat16 [64, 512, 3072], P(('dp', 'blk'), 'uly'), parts along dimension 0, may hold values from -400 to 400
- key_rows: bfloat16 [64, 512, 3072], P(('dp', 'blk'), 'uly'), parts along dimension 0, may hold values from -400 to 400
- value_rows: bfloat16 [64, 512, 3072], P(('dp', 'blk'), 'uly'), parts along dimension 0, may hold values from -6 to 6
- norm_query: float32 [3072], replicated, may hold values from 1 to 2.2
- norm_key: float32 [3072], replicated, may hold values from 1 to 2.2
- out_weight: bfloat16 [3072, 5120], P('blk', 'uly'), may hold values from -0.109375 to 0.109375
- out_bias: float32 [5120], P('uly'), may hold values from -3 to 3
- gate: float32 [5120], P('uly'), may hold values from 0.3 to 1.5
- residual: bfloat16 [64, 512, 5120], P(('dp', 'blk'), None, 'uly'), parts along dimension 0, may hold values from -3 to 3
Outputs:
- mixed: bfloat16 [64, 512, 5120], P(('dp', 'blk'), None, 'uly'), parts along dimension 0
The draws below stay inside these ranges and needn't reach their ends.
There are 8 independent parts, one for each index of `dp`. The reference program is written for one: setup_inputs(seed, part) draws one part's arguments, and reference() takes and returns one part's arrays. A program takes and returns all parts, laid end to end along the dimension named above; an argument that names none is the same for every part. Nothing has to cross between parts.
All inputs are finite; a program needn't handle non-finite values.
Results may differ from the reference program's by a relative error of at most 0.011.
Values may be sent and summed in bfloat16 or wider, within the bound.
No kernel may reach another device: no remote copies, remote signals or barrier semaphores. Data moves between devices by JAX's collectives and lax.ppermute only.
A program may use at most 64 MiB of HBM per device.

```python
import math
import jax
import jax.numpy as jnp
from jax import lax

D = 5120
HEADS = 24
HEAD = 128
HD = 3072
BLOCK = 512
SEQ = 4096
N_BLK = 8


def common_parts(key):
    scales = jnp.exp(jax.random.uniform(jax.random.fold_in(key, 2), (HD,), jnp.float32) * math.log(10.0))
    return scales


def own_rows(key, salt):
    base = jnp.clip(jax.random.normal(jax.random.fold_in(key, salt), (SEQ, HD), jnp.float32), -4.0, 4.0)
    row_scale = jnp.exp(jax.random.uniform(jax.random.fold_in(key, salt + 1), (SEQ, 1), jnp.float32) * math.log(10.0))
    return (base, row_scale)


def draw_query_rows(key, part):
    scales = common_parts(key)
    base, row_scale = own_rows(key, 11)
    drawn = base * row_scale * scales
    return drawn.reshape(N_BLK, BLOCK, HD).astype(jnp.bfloat16)


def draw_key_rows(key, part):
    scales = common_parts(key)
    base, row_scale = own_rows(key, 21)
    drawn = base * row_scale * scales
    return drawn.reshape(N_BLK, BLOCK, HD).astype(jnp.bfloat16)


def block_levels(key, shape, cuts, smallest, largest):
    factor_of = 1.0
    for axis_at, shards_of in cuts:
        draws = jax.random.uniform(jax.random.fold_in(jax.random.fold_in(key, 6), axis_at), (shards_of,), jnp.float32, smallest / len(cuts), largest / len(cuts))
        factor_of = factor_of * jnp.repeat(jnp.exp(draws), shape[axis_at] // shards_of).reshape((-1,) + (1,) * (len(shape) - 1 - axis_at))
    return factor_of


def centred(stream_key, extent, spread, most, pieces=(), kind=jnp.bfloat16):
    result = spread * jax.random.normal(stream_key, extent, jnp.float32)
    if pieces:
        result = result * block_levels(stream_key, extent, pieces, -0.22, 0.18)
    return jnp.clip(result, -most, most).astype(kind)


def setup_inputs(seed: int = 0, part: int = 0) -> dict:
    key_list = jax.random.split(jax.random.key(seed), 10)
    part_keys = jax.random.split(jax.random.fold_in(key_list[9], part), 10)
    return {
        "query_rows": draw_query_rows(jax.random.fold_in(jax.random.fold_in(key_list[9], part), 71), part),
        "key_rows": draw_key_rows(jax.random.fold_in(jax.random.fold_in(key_list[9], part), 71), part),
        "value_rows": centred(part_keys[2], (N_BLK, BLOCK, HD), 1.0, 6.0, ((0, 8), (1, 8))),
        "norm_query": jnp.clip(jnp.exp(jax.random.uniform(key_list[3], (HD,), jnp.float32, math.log(1.0), math.log(2.2))), 1.0, 2.2),
        "norm_key": jnp.clip(jnp.exp(jax.random.uniform(key_list[4], (HD,), jnp.float32, math.log(1.0), math.log(2.2))), 1.0, 2.2),
        "out_weight": centred(key_list[5], (HD, D), HD ** -0.5, 0.109375, ((0, 8), (1, 8))),
        "out_bias": centred(key_list[6], (D,), 0.5, 3.0, ((0, 8),), jnp.float32),
        "gate": jnp.clip(0.3 + 1.2 * jax.random.uniform(key_list[7], (D,), jnp.float32) ** block_levels(key_list[7], (D,), ((0, 8),), -0.2, 0.2), 0.3, 1.5),
        "residual": centred(part_keys[8], (N_BLK, BLOCK, D), 0.5, 3.0, ((0, 8), (2, 8))),
    }


EPS = 1e-06

def normalize(rows_in, gain):
    wide = rows_in.astype(jnp.float32)
    factor = lax.rsqrt(lax.optimization_barrier(jnp.mean(wide * wide, axis=-1, keepdims=True)) + EPS)
    return (wide * factor * gain).astype(jnp.bfloat16)

def one_head(triple):
    queries, keys, values = triple
    scores = jnp.dot(queries, keys.T, preferred_element_type=jnp.float32) * HEAD ** (-0.5)
    peak = lax.optimization_barrier(jnp.max(scores, axis=1, keepdims=True))
    weights = jnp.exp(scores - peak)
    total = lax.optimization_barrier(jnp.sum(weights, axis=1, keepdims=True))
    numer = jnp.dot(weights.astype(jnp.bfloat16), values, preferred_element_type=jnp.float32)
    return (numer / total).astype(jnp.bfloat16)

def flatten(array):
    return array.reshape(SEQ, array.shape[-1])

def split_heads(array):
    return array.reshape(SEQ, HEADS, HEAD).transpose(1, 0, 2)

def reference(query_rows, key_rows, value_rows, norm_query, norm_key, out_weight, out_bias, gate, residual):
    query_norm = normalize(flatten(query_rows), norm_query)
    key_norm = normalize(flatten(key_rows), norm_key)
    values = flatten(value_rows)
    attended = lax.map(one_head, (split_heads(query_norm), split_heads(key_norm), split_heads(values)))
    attended = attended.transpose(1, 0, 2).reshape(SEQ, HD)
    projected = jnp.dot(attended, out_weight, preferred_element_type=jnp.float32)
    mixed = flatten(residual).astype(jnp.float32) + gate * (projected + out_bias)
    return mixed.astype(jnp.bfloat16).reshape(N_BLK, BLOCK, D)
```

```python
import functools

import jax
import jax.numpy as jnp
import numpy as np
from jax import lax
from jax.experimental import pallas as pl
from jax.experimental.pallas import tpu as pltpu
from jax.sharding import Mesh
from jax.sharding import PartitionSpec as P

HEAD = 128
HEADS = 24
EPS = 1e-06
RING = ("yhi", "ylo")
SCALE = HEAD**-0.5 * 1.4426950408889634
F32 = jnp.float32
BF16 = jnp.bfloat16
WHOLE = pl.BlockSpec(memory_space=pltpu.VMEM)
SCALAR = pl.BlockSpec(memory_space=pltpu.SMEM)


def call(kernel, outs, *args, scalars=0, name=None, **extra):
    return pl.pallas_call(
        kernel,
        out_shape=outs,
        in_specs=[SCALAR] * scalars + [WHOLE] * (len(args) - scalars),
        out_specs=jax.tree.map(lambda leaf: WHOLE, outs),
        name=name,
        **extra,
    )(*args)


def norm_kernel(q_ref, k_ref, v_ref, gq_ref, gk_ref, *outs):
    def factor(ref):
        wide = ref[...].astype(F32)
        return lax.rsqrt(jnp.mean(wide * wide, axis=-1, keepdims=True) + EPS)

    fq = factor(q_ref) * SCALE
    fk = factor(k_ref)
    for head in range(HEADS):
        lanes = slice(head * HEAD, head * HEAD + HEAD)
        out = outs[head % 3].at[head // 3]
        out[:, :HEAD] = (q_ref[:, lanes].astype(F32) * fq * gq_ref[:, lanes]).astype(BF16)
        out[:, HEAD : 2 * HEAD] = (k_ref[:, lanes].astype(F32) * fk * gk_ref[:, lanes]).astype(BF16)
        out[:, 2 * HEAD :] = v_ref[:, lanes]


def attend_kernel(r_ref, own_ref, sib_ref, o_ref):
    queries = r_ref[...][:, :, :HEAD].reshape(-1, HEAD)
    rows = queries.shape[0]
    peak = jnp.full((rows, 1), -1e30, F32)
    accum = jnp.zeros((rows, 2 * HEAD), F32)
    for ref in (own_ref, sib_ref):
        for piece in range(ref.shape[0]):
            keys = ref[piece, :, :HEAD]
            values = ref[piece, :, HEAD:]
            values = jnp.concatenate([values, jnp.ones_like(values)], axis=1)
            scores = lax.dot_general(
                queries, keys, (((1,), (1,)), ((), ())), preferred_element_type=F32
            )
            new_peak = jnp.maximum(peak, jnp.max(scores, axis=1, keepdims=True))
            weights = jnp.exp2(scores - new_peak).astype(BF16)
            accum = accum * jnp.exp2(peak - new_peak) + jnp.dot(
                weights, values, preferred_element_type=F32
            )
            peak = new_peak
    out = (accum[:, :HEAD] / accum[:, HEAD : HEAD + 1]).astype(BF16)
    half = rows // 2
    for hi in range(2):
        for lo in range(4):
            o_ref[hi * 4 + lo] = out[hi * half : hi * half + half]


def weight_kernel(at_ref, *refs):
    pieces, out = refs[:-1], refs[-1]
    z, hi = at_ref[0], at_ref[1]
    for far, ref in enumerate(pieces):
        at = lax.rem(z - far + 8, 8)
        for x in range(4):
            for rel in range(2):
                block = x * 2 + (hi + rel) % 2
                for part in range(3):
                    row = at * 48 + part * 16
                    head = row // HEAD
                    dest = pl.multiple_of(head * 1024 + block * HEAD + row % HEAD, 16)
                    out[pl.ds(dest, 16), :] = ref[x, rel * 48 + part * 16 : rel * 48 + part * 16 + 16, :]


def project(a_ref, w_ref, head):
    rows = jnp.concatenate([a_ref[y] for y in range(8)], axis=1)
    return jnp.dot(rows, w_ref[head * 1024 : head * 1024 + 1024, :], preferred_element_type=F32)


def project_kernel(own_ref, sib_ref, w_ref, *refs, head):
    out = refs[-1]
    for side, ref in enumerate((own_ref, sib_ref)):
        total = project(ref, w_ref, head)
        if len(refs) > 1:
            total = total + refs[0][side]
        out[side] = total


def final_kernel(at_ref, own_ref, sib_ref, w_ref, acc_ref, bias_ref, gate_ref, res_ref, o_ref, *, head):
    core = at_ref[0]
    for side, ref in enumerate((own_ref, sib_ref)):
        total = project(ref, w_ref, head) + acc_ref[side]
        total = gate_ref[...] * (total + bias_ref[...])
        for lo in range(4):
            at = pl.multiple_of((2 * lo + (core + side) % 2) * 64, 64)
            wide = res_ref[0, pl.ds(at, 64), :].astype(F32)
            o_ref[0, pl.ds(at, 64), :] = (wide + total[lo * 64 : lo * 64 + 64]).astype(BF16)


def exchange(array, axes):
    return lax.all_to_all(array, axes, split_axis=0, concat_axis=0, tiled=True)


def spread(array, axis, count):
    return exchange(jnp.broadcast_to(array[None], (count,) + array.shape), axis)


def turn(array, axis, count, by):
    return lax.ppermute(array, axis, [(i, (i + by) % count) for i in range(count)])


def after(array, *others):
    return lax.optimization_barrier((array,) + others)[0]


def shards(q, k, v, gain_q, gain_k, weight, bias, gate, residual):
    q, k, v = q[0], k[0], v[0]
    z = lax.axis_index("dp")
    hi = lax.axis_index("yhi")
    core = lax.axis_index("core")

    mine = lax.dynamic_slice(weight, (z * 48, 0), (48, weight.shape[1]))
    theirs = turn(mine, "yhi", 2, 1)
    packs = call(
        norm_kernel,
        [jax.ShapeDtypeStruct((8, 64, 3 * HEAD), BF16)] * 3,
        q, k, v, gain_q[None], gain_k[None], name="norm",
    )
    both = jnp.concatenate([mine, theirs], axis=0)
    local = spread(both, "x", 4)

    got = []
    for head in range(3):
        pack = packs[head]
        if got:
            pack = after(pack, got[-1])
        got.append(exchange(pack, RING))
    attended = []
    own = []
    for head in range(3):
        piece = got[head][:, :, HEAD:].reshape(512, 2 * HEAD)
        if own:
            piece = after(piece, own[-1])
        own.append(spread(piece, "x", 4))
    up, down = [local], [local]
    for step in range(4):
        up.append(turn(up[-1], "dp", 8, 1))
        if step < 3:
            down.append(turn(down[-1], "dp", 8, 7))
    pieces = up + [down[3], down[2], down[1]]
    at = jnp.stack([z, hi]).astype(jnp.int32)
    w = call(
        weight_kernel, jax.ShapeDtypeStruct((3072, weight.shape[1]), BF16), at, *pieces,
        scalars=1, name="assemble",
    )
    acc = None
    for head in range(3):
        other = turn(own[head], "core", 2, 1)
        out = call(
            attend_kernel, jax.ShapeDtypeStruct((8, 256, HEAD), BF16), got[head], own[head], other,
            name="attend",
        )
        if attended:
            out = after(out, attended[-1])
        attended.append(exchange(out, RING))
    width = weight.shape[1]
    for head in range(3):
        other = turn(attended[head], "core", 2, 1)
        if head < 2:
            acc = call(
                functools.partial(project_kernel, head=head),
                jax.ShapeDtypeStruct((2, 256, width), F32),
                attended[head], other, w, *([] if acc is None else [acc]), name="project",
            )
        else:
            return call(
                functools.partial(final_kernel, head=head),
                jax.ShapeDtypeStruct((1, 512, width), BF16),
                core.astype(jnp.int32)[None], attended[head], other, w, acc,
                bias[None], gate[None], residual, scalars=1, name="final",
            )


def solution(mesh):
    split = Mesh(mesh.devices.reshape(8, 4, 2, 4, 2), ("dp", "ylo", "core", "x", "yhi"))
    part, sub = ("dp", "x", "yhi"), ("ylo", "core")
    rows = P(part, sub, None)
    wide = P(part, None, sub)
    placed = (rows, rows, rows, P(), P(), P(("x", "yhi"), sub), P(sub), P(sub), wide)
    return jax.shard_map(shards, mesh=split, in_specs=placed, out_specs=wide, check_vma=False)
```

```python
import functools

import jax
import jax.numpy as jnp
from jax import lax
from jax.experimental import pallas as pl
from jax.experimental.pallas import tpu as pltpu
from jax.sharding import Mesh
from jax.sharding import PartitionSpec as P


HEAD = 128
HEADS = 24
EPS = 1e-06
SCALE = HEAD**-0.5 * 1.4426950408889634
F32 = jnp.float32
BF16 = jnp.bfloat16
WHOLE = pl.BlockSpec(memory_space=pltpu.VMEM)
SCALAR = pl.BlockSpec(memory_space=pltpu.SMEM)


RING = ("yhi", "ylo")


PARAMS = pltpu.CompilerParams(vmem_limit_bytes=24 << 20)


def far_memory(array):
    return pltpu.with_memory_space_constraint(array, pltpu.HBM)


def call(kernel, outs, *args, scalars=0, held=None):
    count = len(args) if held is None else scalars + held
    args = (
        args[:scalars]
        + tuple(pltpu.with_memory_space_constraint(a, pltpu.VMEM) for a in args[scalars:count])
        + tuple(far_memory(a) for a in args[count:])
    )
    return pl.pallas_call(
        kernel,
        out_shape=outs,
        in_specs=[SCALAR] * scalars + [WHOLE] * (len(args) - scalars),
        out_specs=jax.tree.map(lambda leaf: WHOLE, outs),
        compiler_params=PARAMS,
    )(*args)


def factor(ref):
    wide = ref[...].astype(F32)
    return lax.rsqrt(jnp.mean(wide * wide, axis=-1, keepdims=True) + EPS)


def keys_kernel(at_ref, k_ref, v_ref, gain_ref, w_ref, out, quarter):
    start = pl.multiple_of(lax.rem(at_ref[0], 4) * 96, 32)
    quarter[...] = w_ref[pl.ds(start, 96), :]
    scale = factor(k_ref)
    for head in range(HEADS):
        lanes = slice(head * HEAD, head * HEAD + HEAD)
        chip, at = head // 3, head % 3 * 2 * HEAD
        keys = k_ref[:, lanes].astype(F32) * scale * gain_ref[:, lanes]
        out[chip, :, at : at + HEAD] = keys.astype(BF16)
        out[chip, :, at + HEAD : at + 2 * HEAD] = v_ref[:, lanes]


def queries_kernel(q_ref, gain_ref, out):
    scale = factor(q_ref) * SCALE
    for head in range(HEADS):
        lanes = slice(head * HEAD, head * HEAD + HEAD)
        chip, at = head // 3, head % 3 * HEAD
        out[chip, :, at : at + HEAD] = (q_ref[:, lanes].astype(F32) * scale * gain_ref[:, lanes]).astype(BF16)


def absorb(queries, refs, head, peak, accum):
    for ref in refs:
        for start in range(0, ref.shape[0], 512):
            keys = ref[start : start + 512, head * 256 : head * 256 + HEAD]
            values = ref[start : start + 512, head * 256 + HEAD : head * 256 + 256]
            values = jnp.concatenate([values, jnp.ones_like(values)], axis=1)
            scores = lax.dot_general(
                queries, keys, (((1,), (1,)), ((), ())), preferred_element_type=F32
            )
            new_peak = jnp.maximum(peak, jnp.max(scores, axis=1, keepdims=True))
            weights = jnp.exp2(scores - jnp.tile(new_peak, (1, 4))).astype(BF16)
            factor = jnp.tile(jnp.exp2(peak - new_peak), (1, 2))
            accum = accum * factor + jnp.dot(weights, values, preferred_element_type=F32)
            peak = new_peak
    return peak, accum


def query(q_ref, head):
    return q_ref[:, :, head * HEAD : head * HEAD + HEAD].reshape(-1, HEAD)


def attend_kernel(kv_ref, right_ref, left_ref, far_ref, q_ref, out, *, first):
    for head in range(out.shape[0]):
        queries = query(q_ref, first + head)
        rows = queries.shape[0]
        peak = jnp.full((rows, HEAD), -1e30, F32)
        accum = jnp.zeros((rows, 2 * HEAD), F32)
        peak, accum = absorb(queries, (kv_ref, right_ref, left_ref, far_ref), head, peak, accum)
        total = accum[:, HEAD:]
        out[head, :, :HEAD] = accum[:, :HEAD] / total
        out[head, :, HEAD:] = peak + jnp.log2(total)


def merge_kernel(a_ref, b_ref, o_ref):
    for head in range(a_ref.shape[0]):
        one, two = a_ref[head][:, HEAD:], b_ref[head][:, HEAD:]
        top = jnp.maximum(one, two)
        one, two = jnp.exp2(one - top), jnp.exp2(two - top)
        out = (one * a_ref[head][:, :HEAD] + two * b_ref[head][:, :HEAD]) / (one + two)
        out = out.astype(BF16)
        half = out.shape[0] // 2
        for hi in range(2):
            for lo in range(4):
                o_ref[hi * 4 + lo, :, head * HEAD : head * HEAD + HEAD] = out[hi * half : hi * half + half]


def join_kernel(a_ref, b_ref, o_ref):
    rows = a_ref.shape[0]
    o_ref[:rows, :] = a_ref[...]
    o_ref[rows:, :] = b_ref[...]


def weight_kernel(at_ref, *refs):
    pieces, whole, first, rest = refs[:4], refs[4:8], refs[8], refs[9]
    z, x, hi = at_ref[0], at_ref[1], at_ref[2]
    for step, ref in enumerate(whole):
        chip = lax.rem(x + step, 4) * 2 + hi
        first[pl.ds(pl.multiple_of(chip * HEAD, HEAD), HEAD), :] = ref[:HEAD, :]
        rest[pl.ds(pl.multiple_of(chip * 2 * HEAD, HEAD), 2 * HEAD), :] = ref[HEAD:, :]
    flip = x + 1 - 2 * lax.rem(x, 2)
    columns = (x, flip, 3 - x, 3 - flip)
    for back, ref in zip((0, 1, 2, 3), pieces):
        at = lax.rem(z + 4 - back, 4)
        for part in range(3):
            row = at * 96 + part * 32

            def put(out, start, stride, part=part, ref=ref):
                for i, column in enumerate(columns):
                    chip = column * 2 + 1 - hi
                    src = i * 96 + part * 32
                    dest = pl.multiple_of(chip * stride + start, 32)
                    out[pl.ds(dest, 32), :] = ref[src : src + 32, :]

            @pl.when(row < HEAD)
            def _():
                put(first, row, HEAD)

            @pl.when(row >= HEAD)
            def _():
                put(rest, row - HEAD, 2 * HEAD)


def project(ref, w_ref):
    rows = jnp.concatenate([ref[y] for y in range(8)], axis=1)
    return jnp.dot(rows, w_ref[...], preferred_element_type=F32)


def project_kernel(own_ref, sib_ref, w_ref, out):
    for side, ref in enumerate((own_ref, sib_ref)):
        out[side] = project(ref, w_ref)


def mix(at_ref, ref, acc_ref, w_ref, res_ref, bias_ref, gate_ref, side, store):
    core = lax.rem(at_ref[0] + side, 2)
    total = gate_ref[...][None, :] * (project(ref, w_ref) + acc_ref[side] + bias_ref[...][None, :])
    for lo in range(4):
        at = pl.multiple_of((2 * lo + core) * 64, 64)
        rows = slice(lo * 64, lo * 64 + 64)
        store(at, rows, (res_ref[0, pl.ds(at, 64), :].astype(F32) + total[rows]).astype(BF16))


def mine_kernel(at_ref, own_ref, acc_ref, w_ref, res_ref, bias_ref, gate_ref, o_ref):
    def store(at, rows, value):
        o_ref[rows, :] = value

    mix(at_ref, own_ref, acc_ref, w_ref, res_ref, bias_ref, gate_ref, 0, store)


def final_kernel(at_ref, sib_ref, mine_ref, acc_ref, w_ref, res_ref, bias_ref, gate_ref, o_ref):
    for lo in range(4):
        at = pl.multiple_of((2 * lo + at_ref[0]) * 64, 64)
        o_ref[0, pl.ds(at, 64), :] = mine_ref[lo * 64 : lo * 64 + 64, :]

    def store(at, rows, value):
        o_ref[0, pl.ds(at, 64), :] = value

    mix(at_ref, sib_ref, acc_ref, w_ref, res_ref, bias_ref, gate_ref, 1, store)


def exchange(array):
    return lax.all_to_all(array, RING, split_axis=0, concat_axis=0, tiled=True)


SWAP = [(0, 1), (1, 0)]
NEAR = [(i, i ^ 1) for i in range(4)]
FAR = [(i, 3 - i) for i in range(4)]
RIGHT = [(i, (i + 1) % 4) for i in range(4)]
LEFT = [(i, (i + 3) % 4) for i in range(4)]
ACROSS = [(i, (i + 2) % 4) for i in range(4)]
UP = [(i, (i + 1) % 8) for i in range(8)]
DOWN = [(i, (i + 7) % 8) for i in range(8)]


def after(array, *others):
    return lax.optimization_barrier((array,) + others)[0]


def block(q, k, v, gain_q, gain_k, weight, bias, gate, residual):
    q, k, v = q[0], k[0], v[0]
    z, x, hi, core = (lax.axis_index(a).astype(jnp.int32) for a in ("dp", "x", "yhi", "core"))
    width = weight.shape[1]
    at_core = core[None]

    whole = [weight] + [lax.ppermute(weight, "x", [(i, (i + 4 - step) % 4) for i in range(4)]) for step in (1, 2, 3)]
    kv, quarter = call(
        keys_kernel,
        [pltpu.HBM((8, 64, 6 * HEAD), BF16), jax.ShapeDtypeStruct((96, width), BF16)],
        z[None], k, v, gain_k[None], weight, scalars=1, held=0,
    )
    slices = lax.ppermute(quarter, "yhi", SWAP)
    beside = lax.ppermute(slices, "x", NEAR)
    queries = call(queries_kernel, pltpu.HBM((8, 64, 3 * HEAD), BF16), q, gain_q[None], held=0)
    kv = exchange(kv)
    queries = exchange(after(queries, kv))
    rows = kv.reshape(512, 6 * HEAD)
    theirs = lax.ppermute(queries, "core", SWAP)
    attended, ready = [], []
    for i, (first, count) in enumerate(((0, 1), (1, 2))):
        piece = rows[:, first * 256 : (first + count) * 256]
        others = [lax.ppermute(piece, "x", pairs) for pairs in (RIGHT, LEFT, ACROSS)]
        state = jax.ShapeDtypeStruct((count, 512, 2 * HEAD), F32)
        sib_part, own_part = (
            call(functools.partial(attend_kernel, first=first), state, piece, *others, q_part, held=held)
            for q_part, held in ((theirs, 5 - i), (queries, 5))
        )
        out = call(
            merge_kernel, pltpu.HBM((8, 256, count * HEAD), BF16),
            own_part, lax.ppermute(sib_part, "core", SWAP),
        )
        ready.append(out)
        attended.append(exchange(out))
    slices = call(join_kernel, jax.ShapeDtypeStruct((192, width), BF16), slices, beside)
    across = lax.ppermute(slices, "x", FAR)
    pieces = [call(join_kernel, jax.ShapeDtypeStruct((384, width), BF16), slices, across)]
    pieces.append(lax.ppermute(pieces[0], "dp", UP))
    pieces.append(lax.ppermute(pieces[1], "dp", UP))
    pieces.append(lax.ppermute(pieces[0], "dp", DOWN))
    w_first, w_rest = call(
        weight_kernel,
        [jax.ShapeDtypeStruct((1024, width), BF16), jax.ShapeDtypeStruct((2048, width), BF16)],
        jnp.stack([z, x, hi]), *pieces, *whole, scalars=1, held=0,
    )

    sib = [lax.ppermute(attended[i], "core", SWAP) for i in range(2)]
    acc = call(project_kernel, jax.ShapeDtypeStruct((2, 256, width), F32), attended[0], sib[0], w_first)
    rest = (acc, w_rest, residual, bias, gate)
    mixed = call(
        mine_kernel, jax.ShapeDtypeStruct((256, width), BF16), at_core, attended[1], *rest,
        scalars=1, held=4,
    )
    return call(
        final_kernel, jax.ShapeDtypeStruct((1, 512, width), BF16), at_core, sib[1], mixed, *rest,
        scalars=1, held=5,
    )


def solution(mesh):
    split = Mesh(mesh.devices.reshape(8, 4, 2, 4, 2), ("dp", "ylo", "core", "x", "yhi"))
    part, sub = ("dp", "x", "yhi"), ("ylo", "core")
    rows = P(part, sub, None)
    wide = P(part, None, sub)
    placed = (rows, rows, rows, P(), P(), P(("x", "yhi"), sub), P(sub), P(sub), wide)
    return jax.shard_map(block, mesh=split, in_specs=placed, out_specs=wide, check_vma=False)
```
